128 devices in a mesh: row: 8 (over x, z_lo), sim: 16 (over y, z_hi, core).
Axes of the slice: x: 4, y: 4, z: 4 (z_hi: 2, z_lo: 2; z = z_hi * 2 + z_lo), core: 2. Of those that a mesh axis runs over, the one named last changes fastest.
Arguments:
- right_side: float32 [12288, 20480], P('row', 'sim'), may hold values from -6 to 6
- lower_panels: float32 [3, 12288, 512], P(None, ('row', 'sim')), may hold values from -0.15625 to 0.15625
- inverse_blocks: float32 [3, 512, 512], replicated, may hold values from -1 to 1.5, as said below
Outputs:
- solved: float32 [1536, 20480], P('row', 'sim')
- updated: float32 [12288, 20480], P('row', 'sim')
The draws below stay inside these ranges and needn't reach their ends.
Inputs may be any that keep to these rules, and one draw needn't show every extreme that they name: `inverse_blocks`: each block is lower triangular with a diagonal between 0.5 and 1.5.
All inputs are finite; a program needn't handle non-finite values.
Results may differ from the reference program's by a relative error of at most 0.0001.
Values sent between devices are 32-bit elements; how exact they have to be, the bound alone decides.
No kernel may reach another device: no remote copies, remote signals or barrier semaphores. Data moves between devices by JAX's collectives and lax.ppermute only.
A program may use at most 128 MiB of HBM per device.

```python
import jax
import jax.numpy as jnp
from jax import lax

NB = 512
PANELS = 3
BLK_DEV = 3
BLOCKS = 24
SIMS = 20480
N_ROW = 8


def draw_inverse_blocks(key, part):
    first_key, second_key = jax.random.split(jax.random.fold_in(key, 17))
    noise = jnp.clip(jax.random.normal(first_key, (PANELS, NB, NB), jnp.float32), -4.0, 4.0) * (0.5 * NB ** (-0.5))
    diagonal = jax.random.uniform(second_key, (PANELS, NB), jnp.float32, 0.5, 1.5)
    strict = jnp.tril(jnp.ones((NB, NB), jnp.float32), -1)
    identity = jnp.eye(NB, dtype=jnp.float32)
    return noise * strict[None] + diagonal[:, None, :] * identity[None]


def block_scale(stream_key, extent, cuts, least, largest):
    loudness, own = 1.0, jax.random.fold_in(stream_key, 6)
    for position, parts in cuts:
        steps = jnp.exp(jax.random.uniform(jax.random.fold_in(own, position), (parts,), jnp.float32, least / len(cuts), largest / len(cuts)))
        loudness = loudness * jnp.repeat(steps, extent[position] // parts).reshape([-1 if axis == position else 1 for axis in range(len(extent))])
    return loudness


def centred(rng, extent, spread, bound, pieces=(), kind=jnp.bfloat16):
    array = spread * jax.random.normal(rng, extent, jnp.float32)
    if pieces:
        array = array * block_scale(rng, extent, pieces, -0.22, 0.18)
    return jnp.clip(array, -bound, bound).astype(kind)


def setup_inputs(seed: int = 0) -> dict:
    keys = jax.random.split(jax.random.key(seed), 4)
    right_side = centred(keys[0], (BLOCKS * NB, SIMS), 1.0, 6.0, ((0, 8), (1, 16)), jnp.float32)
    lower_panels = centred(keys[1], (PANELS, BLOCKS * NB, NB), (PANELS * NB) ** -0.5, 0.15625, ((1, 128),), jnp.float32)
    inverse_blocks = draw_inverse_blocks(jax.random.fold_in(keys[3], 71), 0)
    return {"right_side": right_side, "lower_panels": lower_panels, "inverse_blocks": inverse_blocks}


def reference(right_side, lower_panels, inverse_blocks):
    sims = right_side.shape[1]
    block_total = BLK_DEV * N_ROW
    blocks = right_side.reshape(N_ROW, BLK_DEV, NB, sims).transpose(1, 0, 2, 3).reshape(block_total, NB, sims)
    factor = lower_panels.reshape(PANELS, N_ROW, BLK_DEV, NB, NB).transpose(0, 2, 1, 3, 4).reshape(PANELS, block_total, NB, NB)
    order = jnp.arange(block_total)
    solved_list = []
    for panel in range(PANELS):
        solved_block = jnp.dot(inverse_blocks[panel], blocks[panel], precision=lax.Precision.HIGHEST, preferred_element_type=jnp.float32)
        solved_list.append(solved_block)
        change = jnp.einsum("bij,jn->bin", factor[panel], solved_block, precision=lax.Precision.HIGHEST)
        keeping = (order > panel).astype(jnp.float32)[:, None, None]
        blocks = blocks - keeping * change
    updated = blocks.reshape(BLK_DEV, N_ROW, NB, sims).transpose(1, 0, 2, 3).reshape(N_ROW * BLK_DEV * NB, sims)
    return jnp.concatenate(solved_list, 0), updated
```

```python
import jax
import jax.numpy as jnp
from jax import lax
from jax.experimental import pallas as pl
from jax.experimental.pallas import tpu as pltpu
from jax.sharding import PartitionSpec as P


NB = 512
PANELS = 3
MAIN, REST = 128, 32
PIECE = MAIN + REST
HALF = PIECE // 2
DEPTH = PANELS * NB
AXES = ("row", "sim")
NT = (((1,), (1,)), ((), ()))


def index_of(x, zl, y, zh, c):
    return (x % 4 * 2 + zl) * 16 + (y % 4 * 4 + zh * 2 + c)


def pairs_of(move):
    pairs = []
    for x in range(4):
        for zl in range(2):
            for y in range(4):
                for zh in range(2):
                    for c in range(2):
                        pairs.append((index_of(x, zl, y, zh, c), index_of(*move(x, zl, y, zh, c))))
    return pairs


X_UP = pairs_of(lambda x, zl, y, zh, c: (x + 1, zl, y, zh, c))
X_DOWN = pairs_of(lambda x, zl, y, zh, c: (x - 1, zl, y, zh, c))
Y_UP = pairs_of(lambda x, zl, y, zh, c: (x, zl, y + 1, zh, c))
Y_DOWN = pairs_of(lambda x, zl, y, zh, c: (x, zl, y - 1, zh, c))
Z_SWAP = pairs_of(lambda x, zl, y, zh, c: (x, 1 - zl, y, zh, c))
FAR_SWAP = pairs_of(lambda x, zl, y, zh, c: (x, zl, y, 1 - zh, c))
CORE_SWAP = pairs_of(lambda x, zl, y, zh, c: (x, zl, y, zh, 1 - c))


def send(array, pairs):
    return lax.ppermute(array, AXES, pairs)


def split(x):
    hi = x.astype(jnp.bfloat16)
    return hi, (x - hi.astype(jnp.float32)).astype(jnp.bfloat16)


def dot3(a, b):
    (ah, al), (bh, bl) = a, b
    dot = lambda u, v: lax.dot_general(u, v, NT, preferred_element_type=jnp.float32)
    return (dot(ah, bl) + dot(al, bh)) + dot(ah, bh)


def spread_rows(lower_panels):
    zeros = jnp.zeros((32, NB), jnp.float32)
    row = lax.axis_index("row")
    held = None
    for k in range(3):
        pairs = [(r * 16 + s, r * 16 + 3 * s + k) for r in (1, 2) for s in range(6) if 3 * s + k < 16]
        got = send(lower_panels[:2, 32 * k : 32 * k + 32], pairs)
        held = got if held is None else held + got
    first = jnp.where(row == 1, held[0], 0.0)
    others = jnp.where(row == 2, held, 0.0)
    rows = jnp.concatenate([first, others[0], others[1]], 0)
    beside = send(rows, [(a, b) for a, b in Z_SWAP if a // 16 in (1, 2)])
    rows = rows + beside
    total = rows
    for k in (1, 2, 3):
        pairs = [((x * 2 + z) * 16 + s, ((x + k) % 4 * 2 + z) * 16 + s) for x in (0, 1) for z in (0, 1) for s in range(16)]
        total = total + send(rows, pairs)
    return total


def over_sim(own):
    far = send(own, FAR_SWAP)
    up, down = send(own, Y_UP), send(own, Y_DOWN)
    g1 = jnp.stack([own, up, down])
    far_up, far_down = send(far, Y_UP), send(far, Y_DOWN)
    g2 = jnp.stack([far, far_up, far_down])
    g3 = jnp.stack([send(up, Y_UP), send(far_down, Y_DOWN)])
    return [g for group in (g1, g2, g3) for g in (group, send(group, CORE_SWAP))]


GROUPS = (
    (((0, 0), (3, 0), (1, 0)), 0), (((0, 0), (3, 0), (1, 0)), 1),
    (((0, 1), (3, 1), (1, 1)), 0), (((0, 1), (3, 1), (1, 1)), 1),
    (((2, 0), (2, 1)), 0), (((2, 0), (2, 1)), 1),
)
SMEM = pl.BlockSpec(memory_space=pltpu.SMEM)
VMEM = pl.BlockSpec(memory_space=pltpu.VMEM)


def members(where_ref, refs):
    y, zh, core = where_ref[2], where_ref[3], where_ref[4]
    for (steps, other), ref in zip(GROUPS, refs):
        c = 1 - core if other else core
        for i, (step, flip) in enumerate(steps):
            z = 1 - zh if flip else zh
            yield ref.at[i], lax.rem(y + step, 4) * 4 + z * 2 + c


def turn_kernel(b_ref, o_ref):
    for d in range(8):
        o_ref[d, :MAIN] = b_ref[:, MAIN * d : MAIN * d + MAIN].T
    rest = b_ref[:, 8 * MAIN :].T
    for d in range(8):
        o_ref[d, MAIN:] = rest[REST * d : REST * d + REST]


def turn(right_side):
    return pl.pallas_call(
        turn_kernel,
        grid=(1,),
        out_shape=jax.ShapeDtypeStruct((8, PIECE, NB), jnp.float32),
        in_specs=[pl.BlockSpec((NB, 1280), lambda i: (0, 0))],
        out_specs=pl.BlockSpec((8, PIECE, NB), lambda i: (0, 0, 0)),
        compiler_params=pltpu.CompilerParams(vmem_limit_bytes=20 << 20),
        cost_estimate=pl.CostEstimate(flops=0, bytes_accessed=5 << 20, transcendentals=0),
        name="turn",
    )(right_side)


def solve_kernel(where_ref, pieces_ref, *refs):
    groups, (inverse_ref, y_ref, wh, wl) = refs[:6], refs[6:]
    for ref, s in members(where_ref, groups):
        rows = pl.ds(pl.multiple_of(s * 32, 32), 32)
        for k in range(3):
            hi, lo = split(ref[32 * k : 32 * k + 32])
            wh[k, rows, :] = hi
            wl[k, rows, :] = lo
    window = lambda k: (wh[k], wl[k])
    y0 = dot3(split(pieces_ref[0]), split(inverse_ref[0]))
    y_ref[:, :NB] = y0
    y0 = split(y0)
    y1 = dot3(split(pieces_ref[1] - dot3(y0, window(0))), split(inverse_ref[1]))
    y_ref[:, NB : 2 * NB] = y1
    y1 = split(y1)
    rest = pieces_ref[2] - dot3(y0, window(1)) - dot3(y1, window(2))
    y_ref[:, 2 * NB :] = dot3(split(rest), split(inverse_ref[2]))


def solve(where, pieces, groups, inverse_blocks):
    whole = lambda p: pl.BlockSpec(p.shape, lambda i: (0,) * len(p.shape))
    return pl.pallas_call(
        solve_kernel,
        grid=(1,),
        out_shape=jax.ShapeDtypeStruct((PIECE, DEPTH), jnp.float32),
        in_specs=[SMEM, pl.BlockSpec((3, PIECE, NB), lambda i: (0, 0, 0))] + [whole(p) for p in (*groups, inverse_blocks)],
        out_specs=pl.BlockSpec((PIECE, DEPTH), lambda i: (0, 0)),
        scratch_shapes=[pltpu.VMEM((3, NB, NB), jnp.bfloat16)] * 2,
        compiler_params=pltpu.CompilerParams(vmem_limit_bytes=30 << 20),
        cost_estimate=pl.CostEstimate(flops=36 * PIECE * NB * NB, bytes_accessed=9 << 20, transcendentals=0),
        name="solve",
    )(where, pieces, *groups, inverse_blocks)


def factor_kernel(where_ref, *refs):
    groups, (h_ref, l_ref) = refs[:6], refs[6:]
    row = where_ref[0]
    for ref, s in members(where_ref, groups):
        first = pl.multiple_of(s * 96, 32)
        rows = pl.ds(first, 96)
        index = first + lax.broadcasted_iota(jnp.int32, (96, NB), 0)
        for k in range(PANELS):
            keep = jnp.logical_or(index >= NB, row > k)
            hi, lo = split(jnp.where(keep, ref[k], 0.0))
            h_ref[rows, k * NB : k * NB + NB] = hi
            l_ref[rows, k * NB : k * NB + NB] = lo


def prepare_factor(where, groups):
    shape = jax.ShapeDtypeStruct((DEPTH, DEPTH), jnp.bfloat16)
    return pl.pallas_call(
        factor_kernel,
        out_shape=(shape, shape),
        in_specs=[SMEM] + [VMEM] * 6,
        out_specs=(VMEM, VMEM),
        compiler_params=pltpu.CompilerParams(vmem_limit_bytes=30 << 20),
        cost_estimate=pl.CostEstimate(flops=4 * DEPTH * DEPTH, bytes_accessed=8 * DEPTH * DEPTH, transcendentals=0),
        name="factor",
    )(where, *groups)


TILE = 512


def put(raw, block, first, ref, rows):
    raw[block, pl.ds(pl.multiple_of(first, 16), rows.stop - rows.start), :] = ref[rows, :]


def update_kernel(fill, where_ref, *refs):
    pieces, (fh, fl, b_ref, _, _, o_ref, s_ref, raw, yh, yl) = refs[:-10], refs[-10:]
    tile, block = pl.program_id(0), pl.program_id(1)

    @pl.when(jnp.logical_and(tile == 0, block == 0))
    def _():
        fill(where_ref, pieces, raw)

    @pl.when(tile == 0)
    def _():
        hi, lo = split(raw[block])
        yh[block] = hi
        yl[block] = lo
        x, z = where_ref[5], where_ref[1]
        start = pl.multiple_of(x * 384 + z * 128, 128)
        turned = raw[block, :, pl.ds(start, 256)].T
        s_ref[...] = jnp.where(z == 0, turned[:192], turned[64:])

    o_ref[...] = b_ref[...] - dot3((fh[...], fl[...]), (yh[block], yl[block]))


def update(blocks, fill, place, where, pieces, factor, right_side, targets):
    whole = lambda p: pl.BlockSpec(p.shape, lambda i, j, w: (0,) * len(p.shape), pipeline_mode=pl.Buffered(1))
    column = pl.BlockSpec((TILE, 256), lambda i, j, w: (i, place(j, w)))
    once = pl.BlockSpec((192, 256), lambda i, j, w: (0, place(jnp.where(i == 0, j, blocks - 1), w)))
    tall = pl.BlockSpec((TILE, DEPTH), lambda i, j, w: (i, 0))
    body = lambda *refs: update_kernel(fill, *refs)
    operands = [where, *pieces, *factor, right_side]
    specs = [whole(p) for p in pieces] + [tall, tall, column]
    aliases = {}
    if targets is None:
        targets = (jnp.zeros((8, 128), jnp.float32),) * 2
    else:
        aliases = {len(operands): 0, len(operands) + 1: 1}
    operands += targets
    specs += [pl.BlockSpec(memory_space=pl.ANY)] * 2
    return pl.pallas_call(
        body,
        out_shape=(jax.ShapeDtypeStruct((1536, 1280), jnp.float32), jax.ShapeDtypeStruct((192, 1280), jnp.float32)),
        grid_spec=pltpu.PrefetchScalarGridSpec(
            num_scalar_prefetch=1,
            grid=(1536 // TILE, blocks),
            in_specs=specs,
            out_specs=(column, once),
            scratch_shapes=[pltpu.VMEM((blocks, 256, DEPTH), d) for d in (jnp.float32, jnp.bfloat16, jnp.bfloat16)],
        ),
        input_output_aliases=aliases,
        compiler_params=pltpu.CompilerParams(vmem_limit_bytes=44 << 20),
        cost_estimate=pl.CostEstimate(
            flops=6 * DEPTH * DEPTH * 256 * blocks,
            bytes_accessed=4 * DEPTH * DEPTH + 3072 * 1024 * blocks, transcendentals=0,
        ),
        name="update",
    )(*operands)


A, B = slice(0, HALF), slice(HALF, PIECE)


def fill_near(where, pieces, raw):
    z = where[1]
    mine, beside = pieces
    put(raw, 0, z * MAIN, mine, slice(0, MAIN))
    put(raw, 0, (1 - z) * MAIN, beside, slice(0, MAIN))


def fill_sides(where, pieces, raw):
    z = where[1]
    left, right, crossed, up, down = pieces
    put(raw, 0, z * MAIN, left, slice(0, MAIN))
    put(raw, 1, z * MAIN, right, slice(0, MAIN))
    other = (1 - z) * MAIN
    put(raw, 0, other, crossed, slice(0, HALF))
    put(raw, 0, other + HALF, up, slice(HALF, MAIN))
    put(raw, 1, other, down, slice(HALF, PIECE))
    put(raw, 1, other + HALF, crossed, slice(HALF, MAIN))


def fill_last(where, pieces, raw):
    x, z = where[5], where[1]
    mine, beside, left, right, crossed, up, down, far_a, far_b = pieces
    put(raw, 0, z * MAIN, up, slice(0, HALF))
    put(raw, 0, z * MAIN + HALF, down, slice(0, MAIN - HALF))
    other = (1 - z) * MAIN
    put(raw, 0, other, far_a, slice(0, HALF))
    put(raw, 0, other + HALF, far_b, slice(0, MAIN - HALF))
    tails = (
        (0, 0, mine, MAIN), (0, 1, beside, MAIN), (3, 0, left, MAIN), (1, 0, right, MAIN),
        (3, 1, up, MAIN), (1, 1, crossed, MAIN), (2, 0, down, MAIN - HALF), (2, 1, far_b, MAIN - HALF),
    )
    for dx, dz, ref, first in tails:
        owner = lax.rem(x + dx, 4) * 2 + (z if dz == 0 else 1 - z)
        put(raw, 1, owner * REST, ref, slice(first, first + REST))


def work(right_side, lower_panels, inverse_blocks):
    row, sim = lax.axis_index("row"), lax.axis_index("sim")
    where = jnp.stack([row, row % 2, sim // 4, sim // 2 % 2, sim % 2, row // 2]).astype(jnp.int32)

    rows = spread_rows(lower_panels)
    window = over_sim(rows)
    factor = prepare_factor(where, over_sim(lower_panels))

    payload = turn(right_side)
    pieces = lax.all_to_all(payload, "row", 0, 0)
    mine = solve(where, pieces, window, inverse_blocks)

    left, right, beside = send(mine, X_UP), send(mine, X_DOWN), send(mine, Z_SWAP)
    crossed = send(jnp.concatenate([left[A], right[B]], 0), Z_SWAP)
    up = send(jnp.concatenate([left[A], beside[B]], 0), X_UP)
    down = send(jnp.concatenate([right[B], beside[A]], 0), X_DOWN)
    far_a, far_b = send(crossed[A], X_UP), send(crossed[B], X_DOWN)

    done = update(1, fill_near, lambda j, w: w[5], where, (mine, beside), factor, right_side, None)
    done = update(
        2, fill_sides, lambda j, w: lax.rem(w[5] + 3 + 2 * j, 4), where, (left, right, crossed, up, down),
        factor, right_side, done,
    )
    done = update(
        2, fill_last, lambda j, w: jnp.where(j == 0, lax.rem(w[5] + 2, 4), 4), where,
        (mine, beside, left, right, crossed, up, down, far_a, far_b), factor, right_side, done,
    )
    return done[1], done[0]


def solution(mesh):
    placed = (P("row", "sim"), P(None, ("row", "sim"), None), P())
    return jax.shard_map(
        work, mesh=mesh, in_specs=placed, out_specs=(P("row", "sim"), P("row", "sim")), check_vma=False
    )
```

```python
import jax
import jax.numpy as jnp
from jax import lax
from jax.experimental import pallas as pl
from jax.experimental.pallas import tpu as pltpu
from jax.sharding import PartitionSpec as P


NB = 512
PANELS = 3
MAIN, REST = 128, 32
PIECE = MAIN + REST
HALF = PIECE // 2
DEPTH = PANELS * NB
AXES = ("row", "sim")
NT = (((1,), (1,)), ((), ()))


def index_of(x, zl, y, zh, c):
    return (x % 4 * 2 + zl) * 16 + (y % 4 * 4 + zh * 2 + c)


def pairs_of(move):
    pairs = []
    for x in range(4):
        for zl in range(2):
            for y in range(4):
                for zh in range(2):
                    for c in range(2):
                        pairs.append((index_of(x, zl, y, zh, c), index_of(*move(x, zl, y, zh, c))))
    return pairs


X_UP = pairs_of(lambda x, zl, y, zh, c: (x + 1, zl, y, zh, c))
X_DOWN = pairs_of(lambda x, zl, y, zh, c: (x - 1, zl, y, zh, c))
Y_UP = pairs_of(lambda x, zl, y, zh, c: (x, zl, y + 1, zh, c))
Y_DOWN = pairs_of(lambda x, zl, y, zh, c: (x, zl, y - 1, zh, c))
Z_SWAP = pairs_of(lambda x, zl, y, zh, c: (x, 1 - zl, y, zh, c))
FAR_SWAP = pairs_of(lambda x, zl, y, zh, c: (x, zl, y, 1 - zh, c))
CORE_SWAP = pairs_of(lambda x, zl, y, zh, c: (x, zl, y, zh, 1 - c))


def send(array, pairs):
    return lax.ppermute(array, AXES, pairs)


def split(x):
    hi = x.astype(jnp.bfloat16)
    return hi, (x - hi.astype(jnp.float32)).astype(jnp.bfloat16)


def dot3(a, b):
    (ah, al), (bh, bl) = a, b
    dot = lambda u, v: lax.dot_general(u, v, NT, preferred_element_type=jnp.float32)
    return (dot(ah, bl) + dot(al, bh)) + dot(ah, bh)


def spread_rows(lower_panels):
    zeros = jnp.zeros((32, NB), jnp.float32)
    row = lax.axis_index("row")
    held = None
    for k in range(3):
        pairs = [(r * 16 + s, r * 16 + 3 * s + k) for r in (1, 2) for s in range(6) if 3 * s + k < 16]
        got = send(lower_panels[:2, 32 * k : 32 * k + 32], pairs)
        held = got if held is None else held + got
    first = jnp.where(row == 1, held[0], 0.0)
    others = jnp.where(row == 2, held, 0.0)
    rows = jnp.concatenate([first, others[0], others[1]], 0)
    beside = send(rows, [(a, b) for a, b in Z_SWAP if a // 16 in (1, 2)])
    rows = rows + beside
    total = rows
    for k in (1, 2, 3):
        pairs = [((x * 2 + z) * 16 + s, ((x + k) % 4 * 2 + z) * 16 + s) for x in (0, 1) for z in (0, 1) for s in range(16)]
        total = total + send(rows, pairs)
    return total


def over_sim(own):
    far = send(own, FAR_SWAP)
    up, down = send(own, Y_UP), send(own, Y_DOWN)
    g1 = jnp.stack([own, up, down])
    far_up, far_down = send(far, Y_UP), send(far, Y_DOWN)
    g2 = jnp.stack([far, far_up, far_down])
    g3 = jnp.stack([send(up, Y_UP), send(far_down, Y_DOWN)])
    return [g for group in (g1, g2, g3) for g in (group, send(group, CORE_SWAP))]


GROUPS = (
    (((0, 0), (3, 0), (1, 0)), 0), (((0, 0), (3, 0), (1, 0)), 1),
    (((0, 1), (3, 1), (1, 1)), 0), (((0, 1), (3, 1), (1, 1)), 1),
    (((2, 0), (2, 1)), 0), (((2, 0), (2, 1)), 1),
)
SMEM = pl.BlockSpec(memory_space=pltpu.SMEM)
VMEM = pl.BlockSpec(memory_space=pltpu.VMEM)


def members(where_ref, refs):
    y, zh, core = where_ref[2], where_ref[3], where_ref[4]
    for (steps, other), ref in zip(GROUPS, refs):
        c = 1 - core if other else core
        for i, (step, flip) in enumerate(steps):
            z = 1 - zh if flip else zh
            yield ref.at[i], lax.rem(y + step, 4) * 4 + z * 2 + c


def turn_kernel(where_ref, b_ref, *refs):
    outs, rest = refs[:-1], refs[-1]
    rest[...] = b_ref[:, 8 * MAIN :].T
    for k, out in enumerate(outs):
        d = lax.rem(where_ref[0] + k, 8)
        out[:MAIN] = b_ref[:, pl.ds(pl.multiple_of(MAIN * d, MAIN), MAIN)].T
        out[MAIN:] = rest[pl.ds(pl.multiple_of(REST * d, REST), REST), :]


def turn(where, right_side):
    piece = jax.ShapeDtypeStruct((PIECE, NB), jnp.float32)
    return pl.pallas_call(
        turn_kernel,
        grid=(1,),
        out_shape=(piece,) * 8,
        in_specs=[SMEM, pl.BlockSpec((NB, 1280), lambda i: (0, 0))],
        out_specs=(pl.BlockSpec((PIECE, NB), lambda i: (0, 0)),) * 8,
        scratch_shapes=[pltpu.VMEM((8 * REST, NB), jnp.float32)],
        compiler_params=pltpu.CompilerParams(vmem_limit_bytes=20 << 20),
        cost_estimate=pl.CostEstimate(flops=0, bytes_accessed=5 << 20, transcendentals=0),
        name="turn",
    )(where, right_side)


def solve_kernel(where_ref, *refs):
    shifted, groups, (inverse_ref, y_ref, raw, wh, wl) = refs[:8], refs[8:14], refs[14:]
    for r in range(PANELS):
        back = lax.rem(where_ref[0] + 8 - r, 8)
        for k, ref in enumerate(shifted):

            @pl.when(back == k)
            def _():
                raw[r] = ref[...]

    for ref, s in members(where_ref, groups):
        rows = pl.ds(pl.multiple_of(s * 32, 32), 32)
        for k in range(3):
            hi, lo = split(ref[32 * k : 32 * k + 32])
            wh[k, rows, :] = hi
            wl[k, rows, :] = lo
    window = lambda k: (wh[k], wl[k])
    y0 = dot3(split(raw[0]), split(inverse_ref[0]))
    y_ref[:, :NB] = y0
    y0 = split(y0)
    y1 = dot3(split(raw[1] - dot3(y0, window(0))), split(inverse_ref[1]))
    y_ref[:, NB : 2 * NB] = y1
    y1 = split(y1)
    rest = raw[2] - dot3(y0, window(1)) - dot3(y1, window(2))
    y_ref[:, 2 * NB :] = dot3(split(rest), split(inverse_ref[2]))


def solve(where, pieces, groups, inverse_blocks):
    whole = lambda p: pl.BlockSpec(p.shape, lambda i: (0,) * len(p.shape))
    return pl.pallas_call(
        solve_kernel,
        grid=(1,),
        out_shape=jax.ShapeDtypeStruct((PIECE, DEPTH), jnp.float32),
        in_specs=[SMEM] + [whole(p) for p in (*pieces, *groups, inverse_blocks)],
        out_specs=pl.BlockSpec((PIECE, DEPTH), lambda i: (0, 0)),
        scratch_shapes=[pltpu.VMEM((3, PIECE, NB), jnp.float32)] + [pltpu.VMEM((3, NB, NB), jnp.bfloat16)] * 2,
        compiler_params=pltpu.CompilerParams(vmem_limit_bytes=34 << 20),
        cost_estimate=pl.CostEstimate(flops=36 * PIECE * NB * NB, bytes_accessed=9 << 20, transcendentals=0),
        name="solve",
    )(where, *pieces, *groups, inverse_blocks)


def factor_kernel(where_ref, *refs):
    groups, (h_ref, l_ref) = refs[:6], refs[6:]
    row = where_ref[0]
    for ref, s in members(where_ref, groups):
        first = pl.multiple_of(s * 96, 32)
        rows = pl.ds(first, 96)
        index = first + lax.broadcasted_iota(jnp.int32, (96, NB), 0)
        for k in range(PANELS):
            keep = jnp.logical_or(index >= NB, row > k)
            hi, lo = split(jnp.where(keep, ref[k], 0.0))
            h_ref[rows, k * NB : k * NB + NB] = hi
            l_ref[rows, k * NB : k * NB + NB] = lo


def prepare_factor(where, groups):
    shape = jax.ShapeDtypeStruct((DEPTH, DEPTH), jnp.bfloat16)
    return pl.pallas_call(
        factor_kernel,
        out_shape=(shape, shape),
        in_specs=[SMEM] + [VMEM] * 6,
        out_specs=(VMEM, VMEM),
        compiler_params=pltpu.CompilerParams(vmem_limit_bytes=30 << 20),
        cost_estimate=pl.CostEstimate(flops=4 * DEPTH * DEPTH, bytes_accessed=8 * DEPTH * DEPTH, transcendentals=0),
        name="factor",
    )(where, *groups)


TILE = 512


def put(raw, block, first, ref, rows):
    raw[block, pl.ds(pl.multiple_of(first, 16), rows.stop - rows.start), :] = ref[rows, :]


def update_kernel(fill, where_ref, *refs):
    pieces, (fh, fl, b_ref, _, _, o_ref, s_ref, raw, yh, yl) = refs[:-10], refs[-10:]
    tile, block = pl.program_id(0), pl.program_id(1)

    @pl.when(jnp.logical_and(tile == 0, block == 0))
    def _():
        fill(where_ref, pieces, raw)

    @pl.when(tile == 0)
    def _():
        hi, lo = split(raw[block])
        yh[block] = hi
        yl[block] = lo
        x, z = where_ref[5], where_ref[1]
        start = pl.multiple_of(x * 384 + z * 128, 128)
        turned = raw[block, :, pl.ds(start, 256)].T
        s_ref[...] = jnp.where(z == 0, turned[:192], turned[64:])

    o_ref[...] = b_ref[...] - dot3((fh[...], fl[...]), (yh[block], yl[block]))


def update(blocks, fill, place, where, pieces, factor, right_side, targets):
    whole = lambda p: pl.BlockSpec(p.shape, lambda i, j, w: (0,) * len(p.shape), pipeline_mode=pl.Buffered(1))
    column = pl.BlockSpec((TILE, 256), lambda i, j, w: (i, place(j, w)))
    once = pl.BlockSpec((192, 256), lambda i, j, w: (0, place(jnp.where(i == 0, j, blocks - 1), w)))
    tall = pl.BlockSpec((TILE, DEPTH), lambda i, j, w: (i, 0))
    body = lambda *refs: update_kernel(fill, *refs)
    operands = [where, *pieces, *factor, right_side]
    specs = [whole(p) for p in pieces] + [tall, tall, column]
    aliases = {}
    if targets is None:
        targets = (jnp.zeros((8, 128), jnp.float32),) * 2
    else:
        aliases = {len(operands): 0, len(operands) + 1: 1}
    operands += targets
    specs += [pl.BlockSpec(memory_space=pl.ANY)] * 2
    return pl.pallas_call(
        body,
        out_shape=(jax.ShapeDtypeStruct((1536, 1280), jnp.float32), jax.ShapeDtypeStruct((192, 1280), jnp.float32)),
        grid_spec=pltpu.PrefetchScalarGridSpec(
            num_scalar_prefetch=1,
            grid=(1536 // TILE, blocks),
            in_specs=specs,
            out_specs=(column, once),
            scratch_shapes=[pltpu.VMEM((blocks, 256, DEPTH), d) for d in (jnp.float32, jnp.bfloat16, jnp.bfloat16)],
        ),
        input_output_aliases=aliases,
        compiler_params=pltpu.CompilerParams(vmem_limit_bytes=44 << 20),
        cost_estimate=pl.CostEstimate(
            flops=6 * DEPTH * DEPTH * 256 * blocks,
            bytes_accessed=4 * DEPTH * DEPTH + 3072 * 1024 * blocks, transcendentals=0,
        ),
        name="update",
    )(*operands)


A, B = slice(0, HALF), slice(HALF, PIECE)


def fill_near(where, pieces, raw):
    z = where[1]
    mine, beside = pieces
    put(raw, 0, z * MAIN, mine, slice(0, MAIN))
    put(raw, 0, (1 - z) * MAIN, beside, slice(0, MAIN))


def fill_sides(where, pieces, raw):
    z = where[1]
    left, right, crossed, up, down = pieces
    put(raw, 0, z * MAIN, left, slice(0, MAIN))
    put(raw, 1, z * MAIN, right, slice(0, MAIN))
    other = (1 - z) * MAIN
    put(raw, 0, other, crossed, slice(0, HALF))
    put(raw, 0, other + HALF, up, slice(HALF, MAIN))
    put(raw, 1, other, down, slice(HALF, PIECE))
    put(raw, 1, other + HALF, crossed, slice(HALF, MAIN))


def fill_last(where, pieces, raw):
    x, z = where[5], where[1]
    mine, beside, left, right, crossed, up, down, far_a, far_b = pieces
    put(raw, 0, z * MAIN, up, slice(0, HALF))
    put(raw, 0, z * MAIN + HALF, down, slice(0, MAIN - HALF))
    other = (1 - z) * MAIN
    put(raw, 0, other, far_a, slice(0, HALF))
    put(raw, 0, other + HALF, far_b, slice(0, MAIN - HALF))
    tails = (
        (0, 0, mine, MAIN), (0, 1, beside, MAIN), (3, 0, left, MAIN), (1, 0, right, MAIN),
        (3, 1, up, MAIN), (1, 1, crossed, MAIN), (2, 0, down, MAIN - HALF), (2, 1, far_b, MAIN - HALF),
    )
    for dx, dz, ref, first in tails:
        owner = lax.rem(x + dx, 4) * 2 + (z if dz == 0 else 1 - z)
        put(raw, 1, owner * REST, ref, slice(first, first + REST))


def work(right_side, lower_panels, inverse_blocks):
    row, sim = lax.axis_index("row"), lax.axis_index("sim")
    where = jnp.stack([row, row % 2, sim // 4, sim // 2 % 2, sim % 2, row // 2]).astype(jnp.int32)

    rows = spread_rows(lower_panels)
    window = over_sim(rows)
    factor = prepare_factor(where, over_sim(lower_panels))

    turned = turn(where, right_side)
    shift = lambda k: [(r * 16 + s, (r + k) % 8 * 16 + s) for r in range(PANELS) for s in range(16)]
    pieces = [turned[0]] + [send(turned[k], shift(k)) for k in range(1, 8)]
    mine = solve(where, pieces, window, inverse_blocks)

    left, right, beside = send(mine, X_UP), send(mine, X_DOWN), send(mine, Z_SWAP)
    crossed = send(jnp.concatenate([left[A], right[B]], 0), Z_SWAP)
    up = send(jnp.concatenate([left[A], beside[B]], 0), X_UP)
    down = send(jnp.concatenate([right[B], beside[A]], 0), X_DOWN)
    far_a, far_b = send(crossed[A], X_UP), send(crossed[B], X_DOWN)

    done = update(1, fill_near, lambda j, w: w[5], where, (mine, beside), factor, right_side, None)
    done = update(
        2, fill_sides, lambda j, w: lax.rem(w[5] + 3 + 2 * j, 4), where, (left, right, crossed, up, down),
        factor, right_side, done,
    )
    done = update(
        2, fill_last, lambda j, w: jnp.where(j == 0, lax.rem(w[5] + 2, 4), 4), where,
        (mine, beside, left, right, crossed, up, down, far_a, far_b), factor, right_side, done,
    )
    return done[1], done[0]


def solution(mesh):
    placed = (P("row", "sim"), P(None, ("row", "sim"), None), P())
    return jax.shard_map(
        work, mesh=mesh, in_specs=placed, out_specs=(P("row", "sim"), P("row", "sim")), check_vma=False
    )
```

```python
import jax
import jax.numpy as jnp
from jax import lax
from jax.experimental import pallas as pl
from jax.experimental.pallas import tpu as pltpu
from jax.sharding import PartitionSpec as P


NB = 512
PANELS = 3
MAIN, REST = 128, 32
PIECE = MAIN + REST
HALF = PIECE // 2
DEPTH = PANELS * NB
AXES = ("row", "sim")
NT = (((1,), (1,)), ((), ()))


def index_of(x, zl, y, zh, c):
    return (x % 4 * 2 + zl) * 16 + (y % 4 * 4 + zh * 2 + c)


def pairs_of(move):
    pairs = []
    for x in range(4):
        for zl in range(2):
            for y in range(4):
                for zh in range(2):
                    for c in range(2):
                        pairs.append((index_of(x, zl, y, zh, c), index_of(*move(x, zl, y, zh, c))))
    return pairs


X_UP = pairs_of(lambda x, zl, y, zh, c: (x + 1, zl, y, zh, c))
X_DOWN = pairs_of(lambda x, zl, y, zh, c: (x - 1, zl, y, zh, c))
Y_UP = pairs_of(lambda x, zl, y, zh, c: (x, zl, y + 1, zh, c))
Y_DOWN = pairs_of(lambda x, zl, y, zh, c: (x, zl, y - 1, zh, c))
Z_SWAP = pairs_of(lambda x, zl, y, zh, c: (x, 1 - zl, y, zh, c))
FAR_SWAP = pairs_of(lambda x, zl, y, zh, c: (x, zl, y, 1 - zh, c))
CORE_SWAP = pairs_of(lambda x, zl, y, zh, c: (x, zl, y, zh, 1 - c))


def send(array, pairs):
    return lax.ppermute(array, AXES, pairs)


def split(x):
    hi = x.astype(jnp.bfloat16)
    return hi, (x - hi.astype(jnp.float32)).astype(jnp.bfloat16)


def dot3(a, b):
    (ah, al), (bh, bl) = a, b
    dot = lambda u, v: lax.dot_general(u, v, NT, preferred_element_type=jnp.float32)
    return (dot(ah, bl) + dot(al, bh)) + dot(ah, bh)


def spread_rows(lower_panels):
    zeros = jnp.zeros((32, NB), jnp.float32)
    row = lax.axis_index("row")
    held = None
    for k in range(3):
        pairs = [(r * 16 + s, r * 16 + 3 * s + k) for r in (1, 2) for s in range(6) if 3 * s + k < 16]
        got = send(lower_panels[:2, 32 * k : 32 * k + 32], pairs)
        held = got if held is None else held + got
    first = jnp.where(row == 1, held[0], 0.0)
    others = jnp.where(row == 2, held, 0.0)
    rows = jnp.concatenate([first, others[0], others[1]], 0)
    beside = send(rows, [(a, b) for a, b in Z_SWAP if a // 16 in (1, 2)])
    rows = rows + beside
    total = rows
    for k in (1, 2, 3):
        pairs = [((x * 2 + z) * 16 + s, ((x + k) % 4 * 2 + z) * 16 + s) for x in (0, 1) for z in (0, 1) for s in range(16)]
        total = total + send(rows, pairs)
    return total


def over_sim(own):
    far = send(own, FAR_SWAP)
    up, down = send(own, Y_UP), send(own, Y_DOWN)
    g1 = jnp.stack([own, up, down])
    far_up, far_down = send(far, Y_UP), send(far, Y_DOWN)
    g2 = jnp.stack([far, far_up, far_down])
    g3 = jnp.stack([send(up, Y_UP), send(far_down, Y_DOWN)])
    return [g for group in (g1, g2, g3) for g in (group, send(group, CORE_SWAP))]


GROUPS = (
    (((0, 0), (3, 0), (1, 0)), 0), (((0, 0), (3, 0), (1, 0)), 1),
    (((0, 1), (3, 1), (1, 1)), 0), (((0, 1), (3, 1), (1, 1)), 1),
    (((2, 0), (2, 1)), 0), (((2, 0), (2, 1)), 1),
)
SMEM = pl.BlockSpec(memory_space=pltpu.SMEM)
VMEM = pl.BlockSpec(memory_space=pltpu.VMEM)


def members(where_ref, refs):
    y, zh, core = where_ref[2], where_ref[3], where_ref[4]
    for (steps, other), ref in zip(GROUPS, refs):
        c = 1 - core if other else core
        for i, (step, flip) in enumerate(steps):
            z = 1 - zh if flip else zh
            yield ref.at[i], lax.rem(y + step, 4) * 4 + z * 2 + c


def turn_kernel(where_ref, b_ref, *refs):
    outs, rest = refs[:-1], refs[-1]
    rest[...] = b_ref[:, 8 * MAIN :].T
    for k, out in enumerate(outs):
        d = lax.rem(where_ref[0] + k, 8)
        out[:MAIN] = b_ref[:, pl.ds(pl.multiple_of(MAIN * d, MAIN), MAIN)].T
        out[MAIN:] = rest[pl.ds(pl.multiple_of(REST * d, REST), REST), :]


def turn(where, right_side):
    piece = jax.ShapeDtypeStruct((PIECE, NB), jnp.float32)
    return pl.pallas_call(
        turn_kernel,
        grid=(1,),
        out_shape=(piece,) * 8,
        in_specs=[SMEM, pl.BlockSpec((NB, 1280), lambda i: (0, 0))],
        out_specs=(pl.BlockSpec((PIECE, NB), lambda i: (0, 0)),) * 8,
        scratch_shapes=[pltpu.VMEM((8 * REST, NB), jnp.float32)],
        compiler_params=pltpu.CompilerParams(vmem_limit_bytes=20 << 20),
        cost_estimate=pl.CostEstimate(flops=0, bytes_accessed=5 << 20, transcendentals=0),
        name="turn",
    )(where, right_side)


def solve_kernel(where_ref, *refs):
    shifted, groups, (inverse_ref, y_ref, raw, wh, wl) = refs[:8], refs[8:14], refs[14:]
    for r in range(PANELS):
        back = lax.rem(where_ref[0] + 8 - r, 8)
        for k, ref in enumerate(shifted):

            @pl.when(back == k)
            def _():
                raw[r] = ref[...]

    for ref, s in members(where_ref, groups):
        rows = pl.ds(pl.multiple_of(s * 32, 32), 32)
        for k in range(3):
            hi, lo = split(ref[32 * k : 32 * k + 32])
            wh[k, rows, :] = hi
            wl[k, rows, :] = lo
    window = lambda k: (wh[k], wl[k])
    y0 = dot3(split(raw[0]), split(inverse_ref[0]))
    y_ref[:, :NB] = y0
    y0 = split(y0)
    y1 = dot3(split(raw[1] - dot3(y0, window(0))), split(inverse_ref[1]))
    y_ref[:, NB : 2 * NB] = y1
    y1 = split(y1)
    rest = raw[2] - dot3(y0, window(1)) - dot3(y1, window(2))
    y_ref[:, 2 * NB :] = dot3(split(rest), split(inverse_ref[2]))


def solve(where, pieces, groups, inverse_blocks):
    whole = lambda p: pl.BlockSpec(p.shape, lambda i: (0,) * len(p.shape))
    return pl.pallas_call(
        solve_kernel,
        grid=(1,),
        out_shape=jax.ShapeDtypeStruct((PIECE, DEPTH), jnp.float32),
        in_specs=[SMEM] + [whole(p) for p in (*pieces, *groups, inverse_blocks)],
        out_specs=pl.BlockSpec((PIECE, DEPTH), lambda i: (0, 0)),
        scratch_shapes=[pltpu.VMEM((3, PIECE, NB), jnp.float32)] + [pltpu.VMEM((3, NB, NB), jnp.bfloat16)] * 2,
        compiler_params=pltpu.CompilerParams(vmem_limit_bytes=34 << 20),
        cost_estimate=pl.CostEstimate(flops=36 * PIECE * NB * NB, bytes_accessed=9 << 20, transcendentals=0),
        name="solve",
    )(where, *pieces, *groups, inverse_blocks)


def factor_kernel(where_ref, *refs):
    groups, (h_ref, l_ref) = refs[:6], refs[6:]
    row = where_ref[0]
    for ref, s in members(where_ref, groups):
        first = pl.multiple_of(s * 96, 32)
        rows = pl.ds(first, 96)
        index = first + lax.broadcasted_iota(jnp.int32, (96, NB), 0)
        for k in range(PANELS):
            keep = jnp.logical_or(index >= NB, row > k)
            hi, lo = split(jnp.where(keep, ref[k], 0.0))
            h_ref[rows, k * NB : k * NB + NB] = hi
            l_ref[rows, k * NB : k * NB + NB] = lo


def prepare_factor(where, groups):
    shape = jax.ShapeDtypeStruct((DEPTH, DEPTH), jnp.bfloat16)
    return pl.pallas_call(
        factor_kernel,
        out_shape=(shape, shape),
        in_specs=[SMEM] + [VMEM] * 6,
        out_specs=(VMEM, VMEM),
        compiler_params=pltpu.CompilerParams(vmem_limit_bytes=30 << 20),
        cost_estimate=pl.CostEstimate(flops=4 * DEPTH * DEPTH, bytes_accessed=8 * DEPTH * DEPTH, transcendentals=0),
        name="factor",
    )(where, *groups)


TILE = 768


def put(raw, block, first, ref, rows):
    raw[block, pl.ds(pl.multiple_of(first, 16), rows.stop - rows.start), :] = ref[rows, :]


def update_kernel(fill, where_ref, *refs):
    pieces, (fh, fl, b_ref, _, _, o_ref, s_ref, raw, yh, yl) = refs[:-10], refs[-10:]
    tile, block = pl.program_id(0), pl.program_id(1)

    @pl.when(jnp.logical_and(tile == 0, block == 0))
    def _():
        fill(where_ref, pieces, raw)

    @pl.when(tile == 0)
    def _():
        hi, lo = split(raw[block])
        yh[block] = hi
        yl[block] = lo
        x, z = where_ref[5], where_ref[1]
        start = pl.multiple_of(x * 384 + z * 128, 128)
        turned = raw[block, :, pl.ds(start, 256)].T
        s_ref[...] = jnp.where(z == 0, turned[:192], turned[64:])

    o_ref[...] = b_ref[...] - dot3((fh[...], fl[...]), (yh[block], yl[block]))


def update(blocks, fill, place, where, pieces, factor, right_side, targets):
    part = lambda n, at: pl.BlockSpec((n, DEPTH), lambda i, j, w: (at, 0), pipeline_mode=pl.Buffered(1))
    column = pl.BlockSpec((TILE, 256), lambda i, j, w: (i, place(j, w)))
    once = pl.BlockSpec((192, 256), lambda i, j, w: (0, place(jnp.where(i == 0, j, blocks - 1), w)))
    tall = pl.BlockSpec((TILE, DEPTH), lambda i, j, w: (i, 0))
    body = lambda *refs: update_kernel(fill, *refs)
    operands = [where, *(p for p, _, _ in pieces), *factor, right_side]
    specs = [part(n, at) for _, n, at in pieces] + [tall, tall, column]
    aliases = {}
    if targets is None:
        targets = (jnp.zeros((8, 128), jnp.float32),) * 2
    else:
        aliases = {len(operands): 0, len(operands) + 1: 1}
    operands += targets
    specs += [pl.BlockSpec(memory_space=pl.ANY)] * 2
    return pl.pallas_call(
        body,
        out_shape=(jax.ShapeDtypeStruct((1536, 1280), jnp.float32), jax.ShapeDtypeStruct((192, 1280), jnp.float32)),
        grid_spec=pltpu.PrefetchScalarGridSpec(
            num_scalar_prefetch=1,
            grid=(1536 // TILE, blocks),
            in_specs=specs,
            out_specs=(column, once),
            scratch_shapes=[pltpu.VMEM((blocks, 256, DEPTH), d) for d in (jnp.float32, jnp.bfloat16, jnp.bfloat16)],
        ),
        input_output_aliases=aliases,
        compiler_params=pltpu.CompilerParams(vmem_limit_bytes=44 << 20),
        cost_estimate=pl.CostEstimate(
            flops=6 * DEPTH * DEPTH * 256 * blocks,
            bytes_accessed=4 * DEPTH * DEPTH + 3072 * 1024 * blocks, transcendentals=0,
        ),
        name="update",
    )(*operands)


A, B = slice(0, HALF), slice(HALF, PIECE)


def fill_near(where, pieces, raw):
    z = where[1]
    mine, beside = pieces
    put(raw, 0, z * MAIN, mine, slice(0, MAIN))
    put(raw, 0, (1 - z) * MAIN, beside, slice(0, MAIN))


def fill_sides(where, pieces, raw):
    z = where[1]
    left, right, crossed, up, down = pieces
    put(raw, 0, z * MAIN, left, slice(0, MAIN))
    put(raw, 1, z * MAIN, right, slice(0, MAIN))
    other = (1 - z) * MAIN
    put(raw, 0, other, crossed, slice(0, HALF))
    put(raw, 0, other + HALF, up, slice(0, MAIN - HALF))
    put(raw, 1, other, down, slice(0, HALF))
    put(raw, 1, other + HALF, crossed, slice(HALF, MAIN))


def fill_last(where, pieces, raw):
    x, z = where[5], where[1]
    mine, beside, left, right, up_tail, crossed, up, down, far_a, far_b = pieces
    put(raw, 0, z * MAIN, up, slice(0, HALF))
    put(raw, 0, z * MAIN + HALF, down, slice(0, MAIN - HALF))
    other = (1 - z) * MAIN
    put(raw, 0, other, far_a, slice(0, HALF))
    put(raw, 0, other + HALF, far_b, slice(0, MAIN - HALF))
    tails = (
        (0, 0, mine, 0), (0, 1, beside, 0), (3, 0, left, 0), (1, 0, right, 0),
        (3, 1, up_tail, 0), (1, 1, crossed, 0), (2, 0, down, MAIN - HALF), (2, 1, far_b, MAIN - HALF),
    )
    for dx, dz, ref, first in tails:
        owner = lax.rem(x + dx, 4) * 2 + (z if dz == 0 else 1 - z)
        put(raw, 1, owner * REST, ref, slice(first, first + REST))


def work(right_side, lower_panels, inverse_blocks):
    row, sim = lax.axis_index("row"), lax.axis_index("sim")
    where = jnp.stack([row, row % 2, sim // 4, sim // 2 % 2, sim % 2, row // 2]).astype(jnp.int32)

    rows = spread_rows(lower_panels)
    window = over_sim(rows)
    factor = prepare_factor(where, over_sim(lower_panels))

    turned = turn(where, right_side)
    shift = lambda k: [(r * 16 + s, (r + k) % 8 * 16 + s) for r in range(PANELS) for s in range(16)]
    pieces = [turned[0]] + [send(turned[k], shift(k)) for k in range(1, 8)]
    mine = solve(where, pieces, window, inverse_blocks)

    left, right, beside = send(mine, X_UP), send(mine, X_DOWN), send(mine, Z_SWAP)
    crossed = send(jnp.concatenate([left[A], right[B]], 0), Z_SWAP)
    up = send(jnp.concatenate([left[A], beside[B]], 0), X_UP)
    down = send(jnp.concatenate([right[B], beside[A]], 0), X_DOWN)
    far_a, far_b = send(crossed[A], X_UP), send(crossed[B], X_DOWN)

    done = update(1, fill_near, lambda j, w: w[5], where, ((mine, MAIN, 0), (beside, MAIN, 0)), factor, right_side, None)
    done = update(
        2, fill_sides, lambda j, w: lax.rem(w[5] + 3 + 2 * j, 4), where,
        ((left, MAIN, 0), (right, MAIN, 0), (crossed, MAIN, 0), (up, HALF, 1), (down, HALF, 1)),
        factor, right_side, done,
    )
    done = update(
        2, fill_last, lambda j, w: jnp.where(j == 0, lax.rem(w[5] + 2, 4), 4), where,
        tuple((p, REST, 4) for p in (mine, beside, left, right, up, crossed))
        + tuple((p, HALF, 0) for p in (up, down, far_a, far_b)), factor, right_side, done,
    )
    return done[1], done[0]


def solution(mesh):
    placed = (P("row", "sim"), P(None, ("row", "sim"), None), P())
    return jax.shard_map(
        work, mesh=mesh, in_specs=placed, out_specs=(P("row", "sim"), P("row", "sim")), check_vma=False
    )
```
